32 devices in a mesh: seq: 8 (over z, y), head: 4 (over x, core).
Axes of the slice: x: 2, y: 2, z: 4, core: 2. Of those that a mesh axis runs over, the one named last changes fastest.
Arguments:
- queries: bfloat16 [8192, 2048], P('seq', 'head'), may hold values from -100 to 100
- values: bfloat16 [8192, 2048], P('seq', 'head'), may hold values from -6 to 6
- codes: int32 [8192, 16], P('seq', 'head'), may hold values from 0 to 511
- codebook: bfloat16 [16, 512, 128], P('head'), may hold values from -4 to 4
- out_weight: bfloat16 [2048, 2048], P('head'), may hold values from -0.125 to 0.125
- grad_out: bfloat16 [8192, 2048], P('seq', 'head'), may hold values from -6 to 6
Outputs:
- grad_queries: bfloat16 [8192, 2048], P('seq', 'head')
- grad_values: bfloat16 [8192, 2048], P('seq', 'head')
- grad_codebook: float32 [16, 512, 128], P('head')
The draws below stay inside these ranges and needn't reach their ends.
All inputs are finite; a program needn't handle non-finite values.
Results may differ from the reference program's by a relative error of at most 0.012.
The reference program's roundings to bfloat16 on the way count: a program that leaves them out, or rounds other values in their place, can miss the bound.
Values may be sent and summed in bfloat16 or wider, within the bound.
A program may use at most 192 MiB of HBM per device.

```python
import math
import jax
import jax.numpy as jnp
import numpy as np
from jax import lax

D = 2048
HEADS = 16
E = 128
S = 512
BLOCK = 512
TOKENS = 8192


def codeword_table(key):
    codewords = jnp.clip(jax.random.normal(jax.random.fold_in(key, 11), (HEADS, S, E), jnp.float32), -4.0, 4.0)
    return codewords


def draw_codebook(key, part):
    return codeword_table(key).astype(jnp.bfloat16)


def draw_queries(key, part):
    queries = jnp.clip(jax.random.normal(jax.random.fold_in(key, 21), (TOKENS, HEADS * E), jnp.float32), -6.0, 6.0)
    return queries.astype(jnp.bfloat16)


def set_ends(values, key, low, high):
    shape = values.shape
    index_at = [jax.random.randint(jax.random.fold_in(key, axis), (), 0, shape[axis]) for axis in range(len(shape))]
    values = values.at[tuple(index_at)].set(low)
    longest = shape.index(max(shape))
    index_at[longest] = (index_at[longest] + 1) % shape[longest]
    return values.at[tuple(index_at)].set(high)


def shard_levels(rng, extent, cuts, least, high):
    level = 1.0
    for axis_at, parts in cuts:
        steps = jax.random.uniform(jax.random.fold_in(jax.random.fold_in(rng, 6), axis_at), (parts,), jnp.float32, least / len(cuts), high / len(cuts))
        level = level * jnp.repeat(jnp.exp(steps), extent[axis_at] // parts).reshape((-1,) + (1,) * (len(extent) - 1 - axis_at))
    return level


def cumulative_ranks(number_of, lean):
    weights = [(1 << 20) // math.isqrt(rank ** lean) + 1 for rank in range(1, number_of + 1)]
    scale = 1 + sum(weights) // (1 << 30)
    return np.cumsum(np.array([max(1, weight // scale) for weight in weights]))


def skewed_ids(key, shape, amount, skew):
    grid = cumulative_ranks(amount, skew)
    ticket = jax.random.randint(jax.random.fold_in(key, 1), shape, 0, int(grid[amount - 1]))
    rank = jnp.searchsorted(jnp.asarray(grid, jnp.int32), ticket, side="right")
    return jax.random.permutation(jax.random.fold_in(key, 2), amount)[rank].astype(jnp.int32)


def scatter_about(key, extent, deviation, most, cuts=(), held_as=jnp.bfloat16):
    result = jax.random.normal(key, extent, jnp.float32) * deviation
    if len(cuts) > 0:
        result = shard_levels(key, extent, cuts, -0.22, 0.18) * result
    return jnp.clip(result, min=-most, max=most).astype(held_as)


def setup_inputs(seed: int = 0) -> dict:
    splits = jax.random.split(jax.random.key(seed), 7)
    queries = draw_queries(jax.random.fold_in(splits[6], 71), 0)
    values = scatter_about(splits[1], (TOKENS, HEADS * E), 1.0, 6.0, ((0, 8), (1, 4)))
    codes = set_ends(skewed_ids(splits[2], (TOKENS, HEADS), S, 2), jax.random.fold_in(splits[2], 3), 0, S - 1).astype(jnp.int32)
    codebook = draw_codebook(jax.random.fold_in(splits[6], 71), 0)
    out_weight = scatter_about(splits[4], (HEADS * E, D), D ** -0.5, 0.125, ((0, 4),))
    grad_out = scatter_about(splits[5], (TOKENS, D), 1.0, 6.0, ((0, 8), (1, 4)))
    return dict(queries=queries, values=values, codes=codes, codebook=codebook, out_weight=out_weight, grad_out=grad_out)


def lowered(array):
    return lax.optimization_barrier(array.astype(jnp.bfloat16)).astype(jnp.float32)


def product(form, left, right):
    return jnp.einsum(form, left.astype(jnp.float32), right.astype(jnp.float32))


def block_terms(query, value, block_codes, dout, codebook, prefix_values, prefix_counts):
    block_rows, heads_all, head_width = query.shape
    entries = codebook.shape[1]
    scale = head_width ** -0.5
    onehot = (block_codes[:, :, None] == jnp.arange(entries, dtype=jnp.int32)[None, None, :]).astype(jnp.float32)
    keys = lowered(product("ths,hse->the", onehot, codebook))
    scores = product("the,uhe->htu", query, keys) * scale
    positions = jnp.arange(block_rows, dtype=jnp.int32)
    causal = positions[:, None] >= positions[None, :]
    cache_scores = product("the,hce->htc", query, codebook) * scale
    counts_row = prefix_counts[:, None, :]
    present = counts_row > 0.0
    highest = jnp.maximum(jnp.max(jnp.where(causal, scores, -jnp.inf), axis=-1, keepdims=True),
                          jnp.max(jnp.where(present, cache_scores, -jnp.inf), axis=-1, keepdims=True))
    local_exp = jnp.where(causal, jnp.exp(jnp.where(causal, scores - highest, 0.0)), 0.0)
    cache_exp = jnp.where(present, jnp.exp(jnp.where(present, cache_scores - highest, 0.0)), 0.0)
    total = jnp.sum(local_exp, axis=-1, keepdims=True) + jnp.sum(cache_exp * counts_row, axis=-1, keepdims=True)
    local_prob = local_exp / total
    cache_prob = cache_exp / total
    local_low = lowered(local_prob)
    cache_low = lowered(cache_prob)
    cache_values = lowered(prefix_values)
    attended = product("htu,uhe->hte", local_low, value) + product("htc,hce->hte", cache_low, cache_values)
    delta = jnp.sum(jnp.transpose(dout.astype(jnp.float32), (1, 0, 2)) * attended, axis=-1)[..., None]
    local_grad = product("the,uhe->htu", dout, value)
    local_score_grad = lowered(local_prob * (local_grad - delta) * scale)
    cache_grad = product("the,hce->htc", dout, cache_values)
    cache_score_grad = lowered(cache_prob * (cache_grad - delta * counts_row) * scale)
    grad_query = (product("htu,uhe->the", local_score_grad, keys)
                  + product("htc,hce->the", cache_score_grad, codebook)).astype(jnp.bfloat16)
    key_grad = lowered(product("htu,the->uhe", local_score_grad, query))
    grad_code = product("ths,the->hse", onehot, key_grad) + product("htc,the->hce", cache_score_grad, query)
    value_part = product("htc,the->hce", cache_low, dout)
    local_values = product("htu,the->uhe", local_low, dout)
    own_values = product("ths,the->hse", onehot, value)
    own_counts = jnp.sum(onehot, axis=0)
    return grad_query, local_values, grad_code, value_part, own_values, own_counts


def reference(queries, values, codes, codebook, out_weight, grad_out):
    heads_all, entries, head_width = codebook.shape
    grad_heads = jnp.dot(grad_out, out_weight.T, preferred_element_type=jnp.float32).astype(jnp.bfloat16)
    nblocks = queries.shape[0] // BLOCK

    def stacked(array):
        return array.reshape(nblocks, BLOCK, heads_all, head_width)

    items = (stacked(queries), stacked(values), codes.reshape(nblocks, BLOCK, heads_all), stacked(grad_heads))

    def forward(carry, item):
        prefix_values, prefix_counts, code_sum = carry
        query, value, block_codes, dout = item
        grad_query, local_values, grad_code, value_part, own_values, own_counts = block_terms(
            query, value, block_codes, dout, codebook, prefix_values, prefix_counts)
        return (prefix_values + own_values, prefix_counts + own_counts, code_sum + grad_code), (grad_query, local_values, value_part)

    start_values = jnp.zeros((heads_all, entries, head_width), jnp.float32)
    start_counts = jnp.zeros((heads_all, entries), jnp.float32)
    (ignored_values, ignored_counts, grad_codebook), (grad_query, local_values, value_parts) = lax.scan(
        forward, (start_values, start_counts, start_values), items)

    def backward(later, item):
        block_codes, local_part, value_part = item
        onehot = (block_codes[:, :, None] == jnp.arange(entries, dtype=jnp.int32)[None, None, :]).astype(jnp.float32)
        lookup = jnp.einsum("ths,hse->the", onehot, lowered(later))
        return later + value_part, (local_part + lookup).astype(jnp.bfloat16)

    ignored_later, grad_value = lax.scan(backward, start_values,
                                         (codes.reshape(nblocks, BLOCK, heads_all), local_values, value_parts), reverse=True)
    return (grad_query.reshape(-1, heads_all * head_width), grad_value.reshape(-1, heads_all * head_width), grad_codebook)
```

```python
import functools

import jax
import jax.numpy as jnp
from jax import lax
from jax.experimental import pallas as pl
from jax.experimental.pallas import tpu as pltpu
from jax.sharding import PartitionSpec as P

BLOCK = 512
CHUNKS = 4
NEG = -1e30
F32 = jnp.float32
BF16 = jnp.bfloat16
MESH = pl.DeviceIdType.MESH


def nn(a, b):
    return lax.dot_general(a, b, (((1,), (0,)), ((), ())), preferred_element_type=F32)


def nt(a, b):
    return lax.dot_general(a, b, (((1,), (1,)), ((), ())), preferred_element_type=F32)


def kernel(
    n_seq, n_head,
    q_ref, v_ref, codes_ref, cb_ref, w_ref, go_ref,
    gq_ref, gv_ref, gc_ref,
    gath, dout, hot_t, hot, keys, keys_t, own, cnt_block, cnt_send, cnt_recv, cnt_before,
    p1_send, p1_recv, p2_send, p2_recv, local_part, vpart, s1_send, s1_recv, s2_send, s2_recv,
    ag_s, ag_r, cn_s, cn_r, p1_s, p1_r, p2_s, p2_r, s1_s, s1_r, s2_s, s2_r,
):
    rows_all = q_ref.shape[0]
    heads, entries, width = cb_ref.shape
    nb = rows_all // BLOCK
    part = entries // n_seq
    scale = width ** (-0.5)
    me = lax.axis_index("seq")
    mine = lax.axis_index("head")
    bits = []
    bit = n_head // 2
    while bit >= 1:
        bits.append(bit)
        bit //= 2

    def flip(index, mask):
        for b in bits:
            if mask & b:
                index = index + b - 2 * b * ((index // b) % 2)
        return index

    barrier = pltpu.get_barrier_semaphore()

    def greet(k, carry):
        pl.semaphore_signal(barrier, inc=1, device_id={"seq": (me + k) % n_seq}, device_id_type=MESH)
        return carry

    lax.fori_loop(1, n_seq, greet, 0)
    for b in bits:
        pl.semaphore_signal(barrier, inc=1, device_id={"head": flip(mine, b)}, device_id_type=MESH)
    pl.semaphore_wait(barrier, n_seq - 1 + len(bits))

    piece = rows_all // CHUNKS

    def gather_copy(src_mask, to, chunk):
        block = flip(mine, src_mask)
        span = pl.ds(chunk * piece, piece)
        src = go_ref.at[span] if src_mask == 0 else gath.at[block, span]
        slot = src_mask ^ to
        return pltpu.make_async_remote_copy(
            src_ref=src, dst_ref=gath.at[block, span],
            send_sem=ag_s.at[slot, chunk], recv_sem=ag_r.at[slot, chunk],
            device_id={"head": flip(mine, to)}, device_id_type=MESH)

    plan = []
    known = [0]
    for b in bits:
        plan += [(m, b) for m in known]
        known += [m ^ b for m in known]
    for m, b in plan:
        if m == 0:
            for chunk in range(CHUNKS):
                gather_copy(m, b, chunk).start()
    by_slot = {m ^ b: (m, b) for m, b in plan}
    taken = set()

    def arrive(slot, chunk):
        if (slot, chunk) not in taken:
            taken.add((slot, chunk))
            m, b = by_slot[slot]
            gather_copy(m, b, chunk).wait_recv()

    def forward(chunk):
        for m, b in plan:
            if m != 0:
                arrive(m, chunk)
                gather_copy(m, b, chunk).start()

    gath[mine] = go_ref[...]

    row_at = lax.broadcasted_iota(jnp.int32, (entries, BLOCK), 0)
    lane_at = lax.broadcasted_iota(jnp.int32, (BLOCK, entries), 1)

    def sums(h, carry):
        head_lanes = pl.ds(pl.multiple_of(h * width, width), width)
        total_values = jnp.zeros((entries, width), F32)
        total_counts = jnp.zeros((1, entries), F32)
        for b in range(nb):
            rows = pl.ds(b * BLOCK, BLOCK)
            code_row = codes_ref[h, :, rows]
            code_full = jnp.transpose(jnp.broadcast_to(code_row, (width, BLOCK)))
            code_cols = jnp.concatenate([code_full] * (entries // width), axis=1)
            one_t = (row_at == code_row).astype(F32).astype(BF16)
            one_f = (lane_at == code_cols).astype(F32)
            one = one_f.astype(BF16)
            hot_t[h, b] = one_t
            hot[h, b] = one
            key = nn(one, cb_ref[h])
            keys[h, b] = key.astype(BF16)
            keys_t[h, b] = jnp.transpose(key).astype(BF16)
            values = nn(one_t, v_ref[rows, head_lanes])
            counts = jnp.sum(one_f, axis=0, keepdims=True)
            own[h, b] = values
            cnt_block[h, b] = counts
            total_values += values
            total_counts += counts
        p1_send[:, h] = total_values.astype(BF16).reshape(n_seq, part, width)
        cnt_send[h] = total_counts
        return carry

    lax.fori_loop(0, heads, sums, 0)

    def count_copy(to, source):
        return pltpu.make_async_remote_copy(
            src_ref=cnt_send, dst_ref=cnt_recv.at[source], send_sem=cn_s.at[to], recv_sem=cn_r.at[source],
            device_id={"seq": to}, device_id_type=MESH)

    def prefix_out(to, source):
        return pltpu.make_async_remote_copy(
            src_ref=p1_send.at[to], dst_ref=p1_recv.at[source], send_sem=p1_s.at[to], recv_sem=p1_r.at[source],
            device_id={"seq": to}, device_id_type=MESH)

    def prefix_back(to, source):
        return pltpu.make_async_remote_copy(
            src_ref=p2_send.at[to], dst_ref=p2_recv.at[source], send_sem=p2_s.at[to], recv_sem=p2_r.at[source],
            device_id={"seq": to}, device_id_type=MESH)

    def over_peers(action):
        def body(k, carry):
            action((me + k) % n_seq)
            return carry

        lax.fori_loop(1, n_seq, body, 0)

    def send_sums(peer):
        prefix_out(peer, me).start()
        count_copy(peer, me).start()

    over_peers(send_sums)
    p1_recv[me] = p1_send[me]
    for chunk in range(CHUNKS // 2):
        forward(chunk)
    over_peers(lambda peer: prefix_out(peer, peer).wait_recv())

    def scan_step(j, total):
        p2_send[j] = total.astype(BF16)
        return total + p1_recv[j].astype(F32)

    lax.fori_loop(0, n_seq, scan_step, jnp.zeros((heads, part, width), F32))
    over_peers(lambda peer: prefix_back(peer, me).start())
    p2_recv[me] = p2_send[me]
    over_peers(lambda peer: count_copy(peer, peer).wait_recv())
    cnt_before[...] = lax.fori_loop(0, me, lambda j, total: total + cnt_recv[j], jnp.zeros(cnt_before.shape, F32))
    for chunk in range(CHUNKS // 2, CHUNKS):
        forward(chunk)
    for chunk in range(CHUNKS):
        for slot in by_slot:
            arrive(slot, chunk)

    depth = go_ref.shape[1]

    def project(r, carry):
        rows = pl.ds(pl.multiple_of(r * BLOCK, BLOCK), BLOCK)
        total = nt(gath[0, rows], w_ref[:, 0:depth])
        for k in range(1, n_head):
            total += nt(gath[k, rows], w_ref[:, k * depth:(k + 1) * depth])
        dout[rows] = total.astype(BF16)
        return carry

    lax.fori_loop(0, nb, project, 0)
    over_peers(lambda peer: prefix_back(peer, peer).wait_recv())

    def late_out(h, to, source):
        return pltpu.make_async_remote_copy(
            src_ref=s1_send.at[h, to], dst_ref=s1_recv.at[h, source],
            send_sem=s1_s.at[h, to], recv_sem=s1_r.at[h, source],
            device_id={"seq": to}, device_id_type=MESH)

    def late_back(h, to, source):
        return pltpu.make_async_remote_copy(
            src_ref=s2_send.at[h, to], dst_ref=s2_recv.at[h, source],
            send_sem=s2_s.at[h, to], recv_sem=s2_r.at[h, source],
            device_id={"seq": to}, device_id_type=MESH)

    def combine(h):
        over_peers(lambda peer: late_out(h, peer, peer).wait_recv())

        def code_step(j, total):
            return total + s1_recv[h, j, 1].astype(F32)

        code = lax.fori_loop(0, n_seq, code_step, jnp.zeros((part, width), F32)).astype(BF16)

        def later_step(k, total):
            j = n_seq - 1 - k
            s2_send[h, j, 0] = total.astype(BF16)
            s2_send[h, j, 1] = code
            return total + s1_recv[h, j, 0].astype(F32)

        lax.fori_loop(0, n_seq, later_step, jnp.zeros((part, width), F32))
        over_peers(lambda peer: late_back(h, peer, me).start())
        s2_recv[h, me] = s2_send[h, me]

    def attend(h, carry):
        head_lanes = pl.ds(pl.multiple_of(h * width, width), width)
        book = cb_ref[h]
        book_t = jnp.transpose(book.astype(F32)).astype(BF16)
        prefix = p2_recv[:, h].astype(F32).reshape(entries, width)
        count_row = cnt_before[h]
        code_total = jnp.zeros((entries, width), F32)
        part_total = jnp.zeros((entries, width), F32)
        for b in range(nb):
            rows = pl.ds(b * BLOCK, BLOCK)
            query = q_ref[rows, head_lanes]
            value = v_ref[rows, head_lanes]
            grad = dout[rows, head_lanes]
            key = keys[h, b]
            cache_values = prefix.astype(BF16)
            count_full = jnp.transpose(jnp.broadcast_to(count_row, (width, entries)))
            bias_full = jnp.where(count_full > 0.0, 0.0, NEG)
            counts = jnp.concatenate([count_full] * (BLOCK // width), axis=1)
            bias = jnp.concatenate([bias_full] * (BLOCK // width), axis=1)
            at_u = lax.broadcasted_iota(jnp.int32, (BLOCK, BLOCK), 0)
            at_t = lax.broadcasted_iota(jnp.int32, (BLOCK, BLOCK), 1)
            scores = jnp.where(at_u <= at_t, nt(key, query) * scale, NEG)
            cache_scores = nt(book, query) * scale + bias
            highest = jnp.maximum(
                jnp.max(scores, axis=0, keepdims=True), jnp.max(cache_scores, axis=0, keepdims=True))
            local_exp = jnp.exp(scores - highest)
            cache_exp = jnp.exp(cache_scores - highest)
            total = jnp.sum(local_exp, axis=0, keepdims=True) + jnp.sum(cache_exp * counts, axis=0, keepdims=True)
            inverse = 1.0 / total
            local_prob = local_exp * inverse
            cache_prob = cache_exp * inverse
            local_low = local_prob.astype(BF16)
            cache_low = cache_prob.astype(BF16)
            local_grad = nt(value, grad)
            cache_grad = nt(cache_values, grad)
            delta = (jnp.sum(local_low.astype(F32) * local_grad, axis=0, keepdims=True)
                     + jnp.sum(cache_low.astype(F32) * cache_grad, axis=0, keepdims=True))
            local_score_grad = (local_prob * (local_grad - delta) * scale).astype(BF16)
            cache_score_grad = (cache_prob * (cache_grad - delta * counts) * scale).astype(BF16)
            gq_t = nn(keys_t[h, b], local_score_grad) + nn(book_t, cache_score_grad)
            gq_ref[rows, head_lanes] = jnp.transpose(gq_t).astype(BF16)
            key_grad = nn(local_score_grad, query).astype(BF16)
            code_total += nn(hot_t[h, b], key_grad) + nn(cache_score_grad, query)
            value_part = nn(cache_low, grad)
            vpart[h, b] = value_part
            part_total += value_part
            local_part[h, b] = nn(local_low, grad)
            prefix = prefix + own[h, b]
            count_row = count_row + cnt_block[h, b]
        s1_send[h, :, 0] = part_total.astype(BF16).reshape(n_seq, part, width)
        s1_send[h, :, 1] = code_total.astype(BF16).reshape(n_seq, part, width)
        s1_recv[h, me] = s1_send[h, me]
        over_peers(lambda peer: late_out(h, peer, me).start())

        @pl.when(h >= 1)
        def _():
            combine(h - 1)

        return carry

    lax.fori_loop(0, heads, attend, 0)
    combine(heads - 1)

    def finish(h, carry):
        head_lanes = pl.ds(pl.multiple_of(h * width, width), width)
        over_peers(lambda peer: late_back(h, peer, peer).wait_recv())
        gc_ref[h] = s2_recv[h, :, 1].astype(F32).reshape(entries, width)
        later = s2_recv[h, :, 0].astype(F32).reshape(entries, width)
        for b in reversed(range(nb)):
            rows = pl.ds(b * BLOCK, BLOCK)
            lookup = nn(hot[h, b], later.astype(BF16))
            gv_ref[rows, head_lanes] = (local_part[h, b] + lookup).astype(BF16)
            later = later + vpart[h, b]
        over_peers(lambda peer: late_out(h, peer, me).wait_send())
        over_peers(lambda peer: late_back(h, peer, me).wait_send())
        return carry

    lax.fori_loop(0, heads, finish, 0)

    def drain(peer):
        prefix_out(peer, me).wait_send()
        prefix_back(peer, me).wait_send()
        count_copy(peer, me).wait_send()

    over_peers(drain)
    for m, b in plan:
        for chunk in range(CHUNKS):
            gather_copy(m, b, chunk).wait_send()


def per_device(queries, values, codes, codebook, out_weight, grad_out):
    n_seq, n_head = lax.axis_size("seq"), lax.axis_size("head")
    row_count = queries.shape[0]
    heads, entries, width = codebook.shape
    nb = row_count // BLOCK
    part = entries // n_seq
    codes_t = codes.T.reshape(heads, 1, row_count)
    vmem = pl.BlockSpec(memory_space=pltpu.VMEM)
    dma = pltpu.SemaphoreType.DMA
    late = pltpu.VMEM((heads, n_seq, 2, part, width), BF16)
    early = pltpu.VMEM((n_seq, heads, part, width), BF16)
    return pl.pallas_call(
        functools.partial(kernel, n_seq, n_head),
        out_shape=(
            jax.ShapeDtypeStruct(queries.shape, BF16),
            jax.ShapeDtypeStruct(queries.shape, BF16),
            jax.ShapeDtypeStruct(codebook.shape, F32),
        ),
        in_specs=[vmem] * 6,
        out_specs=(vmem,) * 3,
        scratch_shapes=[
            pltpu.VMEM((n_head,) + grad_out.shape, BF16),
            pltpu.VMEM(queries.shape, BF16),
            pltpu.VMEM((heads, nb, entries, BLOCK), BF16),
            pltpu.VMEM((heads, nb, BLOCK, entries), BF16),
            pltpu.VMEM((heads, nb, BLOCK, width), BF16),
            pltpu.VMEM((heads, nb, width, BLOCK), BF16),
            pltpu.VMEM((heads, nb, entries, width), F32),
            pltpu.VMEM((heads, nb, 1, entries), F32),
            pltpu.VMEM((heads, 1, entries), F32),
            pltpu.VMEM((n_seq, heads, 1, entries), F32),
            pltpu.VMEM((heads, 1, entries), F32),
            early, early, early, early,
            pltpu.VMEM((heads, nb, BLOCK, width), F32),
            pltpu.VMEM((heads, nb, entries, width), F32),
            late, late, late, late,
            dma((n_head, CHUNKS)), dma((n_head, CHUNKS)),
            dma((n_seq,)), dma((n_seq,)),
            dma((n_seq,)), dma((n_seq,)),
            dma((n_seq,)), dma((n_seq,)),
            dma((heads, n_seq)), dma((heads, n_seq)),
            dma((heads, n_seq)), dma((heads, n_seq)),
        ],
        compiler_params=pltpu.CompilerParams(
            collective_id=0, has_side_effects=True, vmem_limit_bytes=60 * 1024 * 1024),
    )(queries, values, codes_t, codebook, out_weight, grad_out)


def solution(mesh):
    return jax.shard_map(
        per_device,
        mesh=mesh,
        in_specs=(
            P("seq", "head"),
            P("seq", "head"),
            P("seq", "head"),
            P("head", None, None),
            P("head", None),
            P("seq", "head"),
        ),
        out_specs=(P("seq", "head"), P("seq", "head"), P("head", None, None)),
        check_vma=False,
    )
```

```python
import functools
import math

import jax
import jax.numpy as jnp
from jax import lax
from jax.experimental import pallas as pl
from jax.experimental.pallas import tpu as pltpu
from jax.sharding import PartitionSpec as P

BLOCK = 512
HALF = BLOCK // 2
NEG = -1e30
F32 = jnp.float32
BF16 = jnp.bfloat16
MESH = pl.DeviceIdType.MESH


def nn(a, b):
    return lax.dot_general(a, b, (((1,), (0,)), ((), ())), preferred_element_type=F32)


def nt(a, b):
    return lax.dot_general(a, b, (((1,), (1,)), ((), ())), preferred_element_type=F32)


def kernel(
    n_seq, n_head,
    q_ref, v_ref, codes_ref, cb_ref, w_ref, go_ref,
    gq_ref, gv_ref, gc_ref,
    gath, dout, hot_t, hot, keys, keys_t, own, cnt_block, cnt_send, cnt_recv, cnt_before,
    counts_at, low, cache_low, local_part, vpart,
    p1_send, p1_recv, p2_send, p2_recv, l1_send, l1_recv, l2_send, l2_recv, s1_send, s1_recv, s2_send, s2_recv,
    ag_s, ag_r, cn_s, cn_r, p1_s, p1_r, p2_s, p2_r, l1_s, l1_r, l2_s, l2_r, s1_s, s1_r, s2_s, s2_r,
):
    rows_all = q_ref.shape[0]
    heads, entries, width = cb_ref.shape
    nb = rows_all // BLOCK
    part = entries // n_seq
    scale = width ** (-0.5)
    me = lax.axis_index("seq")
    mine = lax.axis_index("head")
    bits = []
    bit = n_head // 2
    while bit >= 1:
        bits.append(bit)
        bit //= 2

    def flip(index, mask):
        for b in bits:
            if mask & b:
                index = index + b - 2 * b * ((index // b) % 2)
        return index

    barrier = pltpu.get_barrier_semaphore()

    def greet(k, carry):
        pl.semaphore_signal(barrier, inc=1, device_id={"seq": (me + k) % n_seq}, device_id_type=MESH)
        return carry

    lax.fori_loop(1, n_seq, greet, 0)
    for b in bits:
        pl.semaphore_signal(barrier, inc=1, device_id={"head": flip(mine, b)}, device_id_type=MESH)
    pl.semaphore_wait(barrier, n_seq - 1 + len(bits))

    chunks = heads
    piece = rows_all // chunks

    def gather_copy(src_mask, to, chunk):
        block = flip(mine, src_mask)
        span = pl.ds(chunk * piece, piece)
        src = go_ref.at[span] if src_mask == 0 else gath.at[block, span]
        slot = src_mask ^ to
        return pltpu.make_async_remote_copy(
            src_ref=src, dst_ref=gath.at[block, span],
            send_sem=ag_s.at[slot, chunk], recv_sem=ag_r.at[slot, chunk],
            device_id={"head": flip(mine, to)}, device_id_type=MESH)

    plan = []
    known = [0]
    for b in bits:
        plan += [(m, b) for m in known]
        known += [m ^ b for m in known]
    for m, b in plan:
        if m == 0:
            for chunk in range(chunks):
                gather_copy(m, b, chunk).start()
    relayed = {m for m, b in plan if m != 0}

    def forward(chunk):
        done = set()
        for m, b in plan:
            if m != 0:
                if m not in done:
                    done.add(m)
                    first, to = next((x, y) for x, y in plan if x ^ y == m)
                    gather_copy(first, to, chunk).wait_recv()
                gather_copy(m, b, chunk).start()

    gath[mine] = go_ref[...]

    row_at = lax.broadcasted_iota(jnp.int32, (entries, BLOCK), 0)
    lane_at = lax.broadcasted_iota(jnp.int32, (BLOCK, entries), 1)

    def sums(h, carry):
        head_lanes = pl.ds(pl.multiple_of(h * width, width), width)
        total_values = jnp.zeros((entries, width), F32)
        total_counts = jnp.zeros((1, entries), F32)
        for b in range(nb):
            rows = pl.ds(b * BLOCK, BLOCK)
            code_row = codes_ref[h, :, rows]
            code_full = jnp.transpose(jnp.broadcast_to(code_row, (width, BLOCK)))
            code_cols = jnp.concatenate([code_full] * (entries // width), axis=1)
            one_t = (row_at == code_row).astype(F32).astype(BF16)
            one_f = (lane_at == code_cols).astype(F32)
            one = one_f.astype(BF16)
            hot_t[h, b] = one_t
            hot[h, b] = one
            key = nn(one, cb_ref[h])
            keys[h, b] = key.astype(BF16)
            keys_t[h, b] = jnp.transpose(key).astype(BF16)
            values = nn(one_t, v_ref[rows, head_lanes])
            counts = jnp.sum(one_f, axis=0, keepdims=True)
            own[h, b] = values
            cnt_block[h, b] = counts
            total_values += values
            total_counts += counts
        p1_send[:, h] = total_values.astype(BF16).reshape(n_seq, part, width)
        cnt_send[h] = total_counts
        return carry

    lax.fori_loop(0, heads, sums, 0)

    def count_copy(to, source):
        return pltpu.make_async_remote_copy(
            src_ref=cnt_send, dst_ref=cnt_recv.at[source], send_sem=cn_s.at[to], recv_sem=cn_r.at[source],
            device_id={"seq": to}, device_id_type=MESH)

    def prefix_out(to, source):
        return pltpu.make_async_remote_copy(
            src_ref=p1_send.at[to], dst_ref=p1_recv.at[source], send_sem=p1_s.at[to], recv_sem=p1_r.at[source],
            device_id={"seq": to}, device_id_type=MESH)

    def prefix_back(to, source):
        return pltpu.make_async_remote_copy(
            src_ref=p2_send.at[to], dst_ref=p2_recv.at[source], send_sem=p2_s.at[to], recv_sem=p2_r.at[source],
            device_id={"seq": to}, device_id_type=MESH)

    def over_peers(action):
        def body(k, carry):
            action((me + k) % n_seq)
            return carry

        lax.fori_loop(1, n_seq, body, 0)

    def send_sums(peer):
        prefix_out(peer, me).start()
        count_copy(peer, me).start()

    over_peers(send_sums)
    p1_recv[me] = p1_send[me]
    over_peers(lambda peer: count_copy(peer, peer).wait_recv())
    cnt_before[...] = lax.fori_loop(0, me, lambda j, total: total + cnt_recv[j], jnp.zeros(cnt_before.shape, F32))

    def scan_step(j, total):
        p2_send[j] = total.astype(BF16)
        return total + p1_recv[j].astype(F32)

    def scan_prefix():
        over_peers(lambda peer: prefix_out(peer, peer).wait_recv())
        lax.fori_loop(0, n_seq, scan_step, jnp.zeros((heads, part, width), F32))
        over_peers(lambda peer: prefix_back(peer, me).start())
        p2_recv[me] = p2_send[me]

    tri = (lax.broadcasted_iota(jnp.int32, (HALF, HALF), 0) <= lax.broadcasted_iota(jnp.int32, (HALF, HALF), 1))
    rate = scale * math.log2(math.e)

    def wide(column):
        return jnp.concatenate([column] * (HALF // width), axis=1)

    def probabilities(h, carry):
        head_lanes = pl.ds(pl.multiple_of(h * width, width), width)
        book = cb_ref[h]
        count_row = cnt_before[h]
        for b in range(nb):
            count_full = jnp.transpose(jnp.broadcast_to(count_row, (width, entries)))
            counts_at[h, b] = count_full
            counts = wide(count_full)
            bias = wide(jnp.where(count_full > 0.0, 0.0, NEG))
            for half in range(2):
                upto = (half + 1) * HALF
                cols = pl.ds(half * HALF, HALF)
                query = q_ref[pl.ds(b * BLOCK + half * HALF, HALF), head_lanes]
                diagonal = jnp.where(tri, nt(keys[h, b, half * HALF:upto], query), NEG)
                cache_scores = nt(book, query) + bias
                highest = jnp.maximum(
                    jnp.max(diagonal, axis=0, keepdims=True), jnp.max(cache_scores, axis=0, keepdims=True))
                if half:
                    above = nt(keys[h, b, 0:HALF], query)
                    highest = jnp.maximum(highest, jnp.max(above, axis=0, keepdims=True))
                    above_exp = jnp.exp2((above - highest) * rate)
                diagonal_exp = jnp.exp2((diagonal - highest) * rate)
                cache_exp = jnp.exp2((cache_scores - highest) * rate)
                total = (jnp.sum(diagonal_exp, axis=0, keepdims=True)
                         + jnp.sum(cache_exp * counts, axis=0, keepdims=True))
                if half:
                    total = total + jnp.sum(above_exp, axis=0, keepdims=True)
                inverse = 1.0 / total
                low[h, b, half * HALF:upto, cols] = (diagonal_exp * inverse).astype(BF16)
                if half:
                    low[h, b, 0:HALF, cols] = (above_exp * inverse).astype(BF16)
                cache_low[h, b, :, cols] = (cache_exp * inverse).astype(BF16)
            count_row = count_row + cnt_block[h, b]
        forward(h)

        @pl.when(h == max(heads - 2, 0))
        def _():
            scan_prefix()

        return carry

    lax.fori_loop(0, heads, probabilities, 0)
    for chunk in range(chunks):
        for m, b in plan:
            if m ^ b not in relayed:
                gather_copy(m, b, chunk).wait_recv()

    depth = go_ref.shape[1]

    def project(r, carry):
        rows = pl.ds(pl.multiple_of(r * BLOCK, BLOCK), BLOCK)
        total = nt(gath[0, rows], w_ref[:, 0:depth])
        for k in range(1, n_head):
            total += nt(gath[k, rows], w_ref[:, k * depth:(k + 1) * depth])
        dout[rows] = total.astype(BF16)
        return carry

    lax.fori_loop(0, nb, project, 0)

    def cache_parts(h, carry):
        head_lanes = pl.ds(pl.multiple_of(h * width, width), width)
        part_total = jnp.zeros((entries, width), F32)
        for b in range(nb):
            value_part = nn(cache_low[h, b], dout[pl.ds(b * BLOCK, BLOCK), head_lanes])
            vpart[h, b] = value_part
            part_total += value_part
        l1_send[:, h] = part_total.astype(BF16).reshape(n_seq, part, width)
        return carry

    lax.fori_loop(0, heads, cache_parts, 0)

    def suffix_out(to, source):
        return pltpu.make_async_remote_copy(
            src_ref=l1_send.at[to], dst_ref=l1_recv.at[source], send_sem=l1_s.at[to], recv_sem=l1_r.at[source],
            device_id={"seq": to}, device_id_type=MESH)

    def suffix_back(to, source):
        return pltpu.make_async_remote_copy(
            src_ref=l2_send.at[to], dst_ref=l2_recv.at[source], send_sem=l2_s.at[to], recv_sem=l2_r.at[source],
            device_id={"seq": to}, device_id_type=MESH)

    over_peers(lambda peer: suffix_out(peer, me).start())
    l1_recv[me] = l1_send[me]

    def later_step(k, total):
        j = n_seq - 1 - k
        l2_send[j] = total.astype(BF16)
        return total + l1_recv[j].astype(F32)

    def scan_suffix():
        over_peers(lambda peer: suffix_out(peer, peer).wait_recv())
        lax.fori_loop(0, n_seq, later_step, jnp.zeros((heads, part, width), F32))
        over_peers(lambda peer: suffix_back(peer, me).start())
        l2_recv[me] = l2_send[me]

    over_peers(lambda peer: prefix_back(peer, peer).wait_recv())

    def late_out(h, to, source):
        return pltpu.make_async_remote_copy(
            src_ref=s1_send.at[h, to], dst_ref=s1_recv.at[h, source],
            send_sem=s1_s.at[h, to], recv_sem=s1_r.at[h, source],
            device_id={"seq": to}, device_id_type=MESH)

    def late_back(h, to, source):
        return pltpu.make_async_remote_copy(
            src_ref=s2_send.at[h], dst_ref=s2_recv.at[h, source],
            send_sem=s2_s.at[h, to], recv_sem=s2_r.at[h, source],
            device_id={"seq": to}, device_id_type=MESH)

    def combine(h):
        over_peers(lambda peer: late_out(h, peer, peer).wait_recv())

        def code_step(j, total):
            return total + s1_recv[h, j].astype(F32)

        s2_send[h] = lax.fori_loop(0, n_seq, code_step, jnp.zeros((part, width), F32)).astype(BF16)
        over_peers(lambda peer: late_back(h, peer, me).start())
        s2_recv[h, me] = s2_send[h]

    def attend(h, carry):
        head_lanes = pl.ds(pl.multiple_of(h * width, width), width)
        book = cb_ref[h]
        book_t = jnp.transpose(book.astype(F32)).astype(BF16)
        prefix = p2_recv[:, h].astype(F32).reshape(entries, width)
        from_cache = jnp.zeros((entries, width), F32)
        from_keys = jnp.zeros((entries, width), F32)
        for b in range(nb):
            cache_values = prefix.astype(BF16)
            counts = wide(counts_at[h, b])
            key_parts = []
            value_parts = []
            for half in range(2):
                upto = (half + 1) * HALF
                cols = pl.ds(half * HALF, HALF)
                rows = pl.ds(b * BLOCK + half * HALF, HALF)
                query = q_ref[rows, head_lanes]
                grad = dout[rows, head_lanes]
                local_grad = nt(v_ref[pl.ds(b * BLOCK, upto), head_lanes], grad)
                cache_grad = nt(cache_values, grad)
                local_low = low[h, b, 0:upto, cols]
                local_prob = local_low.astype(F32)
                cache_prob = cache_low[h, b, :, cols].astype(F32)
                delta = (jnp.sum(local_prob * local_grad, axis=0, keepdims=True)
                         + jnp.sum(cache_prob * cache_grad, axis=0, keepdims=True))
                local_score_grad = (local_prob * (local_grad - delta)).astype(BF16)
                cache_score_grad = (cache_prob * (cache_grad - delta * counts)).astype(BF16)
                gq_t = nn(keys_t[h, b, :, 0:upto], local_score_grad) + nn(book_t, cache_score_grad)
                gq_ref[rows, head_lanes] = jnp.transpose(gq_t * scale).astype(BF16)
                key_parts.append(nn(local_score_grad, query))
                value_parts.append(nn(local_low, grad))
                from_cache += nn(cache_score_grad, query)
            for at, parts in enumerate((key_parts, value_parts)):
                joined = jnp.concatenate([parts[0] + parts[1][:HALF], parts[1][HALF:]], axis=0)
                if at:
                    local_part[h, b] = joined
                else:
                    from_keys += nn(hot_t[h, b], (joined * scale).astype(BF16))
            prefix = prefix + own[h, b]
        s1_send[h] = (from_keys + from_cache * scale).astype(BF16).reshape(n_seq, part, width)
        s1_recv[h, me] = s1_send[h, me]
        over_peers(lambda peer: late_out(h, peer, me).start())

        @pl.when(h == min(1, heads - 1))
        def _():
            scan_suffix()

        @pl.when(h >= 1)
        def _():
            combine(h - 1)

        return carry

    lax.fori_loop(0, heads, attend, 0)
    over_peers(lambda peer: suffix_back(peer, peer).wait_recv())

    def finish(h, carry):
        head_lanes = pl.ds(pl.multiple_of(h * width, width), width)
        later = l2_recv[:, h].astype(F32).reshape(entries, width)
        for b in reversed(range(nb)):
            rows = pl.ds(b * BLOCK, BLOCK)
            lookup = nn(hot[h, b], later.astype(BF16))
            gv_ref[rows, head_lanes] = (local_part[h, b] + lookup).astype(BF16)
            later = later + vpart[h, b]

        @pl.when(h == heads - 2)
        def _():
            combine(heads - 1)

        return carry

    lax.fori_loop(0, heads, finish, 0)
    if heads == 1:
        combine(0)

    def release(h, carry):
        over_peers(lambda peer: late_back(h, peer, peer).wait_recv())
        gc_ref[h] = s2_recv[h].astype(F32).reshape(entries, width)
        over_peers(lambda peer: late_out(h, peer, me).wait_send())
        over_peers(lambda peer: late_back(h, peer, me).wait_send())
        return carry

    lax.fori_loop(0, heads, release, 0)

    def drain(peer):
        prefix_out(peer, me).wait_send()
        prefix_back(peer, me).wait_send()
        count_copy(peer, me).wait_send()
        suffix_out(peer, me).wait_send()
        suffix_back(peer, me).wait_send()

    over_peers(drain)
    for m, b in plan:
        for chunk in range(chunks):
            gather_copy(m, b, chunk).wait_send()


def per_device(queries, values, codes, codebook, out_weight, grad_out):
    n_seq, n_head = lax.axis_size("seq"), lax.axis_size("head")
    row_count = queries.shape[0]
    heads, entries, width = codebook.shape
    nb = row_count // BLOCK
    part = entries // n_seq
    codes_t = codes.T.reshape(heads, 1, row_count)
    vmem = pl.BlockSpec(memory_space=pltpu.VMEM)
    dma = pltpu.SemaphoreType.DMA
    late = pltpu.VMEM((heads, n_seq, part, width), BF16)
    early = pltpu.VMEM((n_seq, heads, part, width), BF16)
    return pl.pallas_call(
        functools.partial(kernel, n_seq, n_head),
        out_shape=(
            jax.ShapeDtypeStruct(queries.shape, BF16),
            jax.ShapeDtypeStruct(queries.shape, BF16),
            jax.ShapeDtypeStruct(codebook.shape, F32),
        ),
        in_specs=[vmem] * 6,
        out_specs=(vmem,) * 3,
        scratch_shapes=[
            pltpu.VMEM((n_head,) + grad_out.shape, BF16),
            pltpu.VMEM(queries.shape, BF16),
            pltpu.VMEM((heads, nb, entries, BLOCK), BF16),
            pltpu.VMEM((heads, nb, BLOCK, entries), BF16),
            pltpu.VMEM((heads, nb, BLOCK, width), BF16),
            pltpu.VMEM((heads, nb, width, BLOCK), BF16),
            pltpu.VMEM((heads, nb, entries, width), F32),
            pltpu.VMEM((heads, nb, 1, entries), F32),
            pltpu.VMEM((heads, 1, entries), F32),
            pltpu.VMEM((n_seq, heads, 1, entries), F32),
            pltpu.VMEM((heads, 1, entries), F32),
            pltpu.VMEM((heads, nb, entries, width), F32),
            pltpu.VMEM((heads, nb, BLOCK, BLOCK), BF16),
            pltpu.VMEM((heads, nb, entries, BLOCK), BF16),
            pltpu.VMEM((heads, nb, BLOCK, width), F32),
            pltpu.VMEM((heads, nb, entries, width), F32),
            early, early, early, early,
            early, early, early, early,
            late, late, pltpu.VMEM((heads, part, width), BF16), late,
            dma((n_head, heads)), dma((n_head, heads)),
            dma((n_seq,)), dma((n_seq,)),
            dma((n_seq,)), dma((n_seq,)),
            dma((n_seq,)), dma((n_seq,)),
            dma((n_seq,)), dma((n_seq,)),
            dma((n_seq,)), dma((n_seq,)),
            dma((heads, n_seq)), dma((heads, n_seq)),
            dma((heads, n_seq)), dma((heads, n_seq)),
        ],
        compiler_params=pltpu.CompilerParams(
            collective_id=0, has_side_effects=True, vmem_limit_bytes=60 * 1024 * 1024),
    )(queries, values, codes_t, codebook, out_weight, grad_out)


def solution(mesh):
    return jax.shard_map(
        per_device,
        mesh=mesh,
        in_specs=(
            P("seq", "head"),
            P("seq", "head"),
            P("seq", "head"),
            P("head", None, None),
            P("head", None),
            P("seq", "head"),
        ),
        out_specs=(P("seq", "head"), P("seq", "head"), P("head", None, None)),
        check_vma=False,
    )
```
